256 devices in a mesh: section: 4 (over x_hi, core), tile: 64 (over z, x_lo, y).
Axes of the slice: x: 4 (x_hi: 2, x_lo: 2; x = x_hi * 2 + x_lo), y: 4, z: 8, core: 2. Of those that a mesh axis runs over, the one named last changes fastest.
Arguments:
- saved: float32 [4, 5, 8, 512, 128], P('section', None, None, 'tile'), may hold values from -2.5 to 2.5
- sched: int32 [4], replicated, may hold values from 0 to 3, each once
Outputs:
- gradient: float32 [5, 8, 512, 128], P(None, None, 'tile')
The draws below stay inside these ranges and needn't reach their ends.
Inputs may be any that keep to these rules, and one draw needn't show every extreme that they name: sched is a permutation of 0 .. 3.
All inputs are finite; a program needn't handle non-finite values.
Results may differ from the reference program's by a relative error of at most 0.0001.
Values sent between devices are 32-bit elements; how exact they have to be, the bound alone decides.
A program may use at most 64 MiB of HBM per device.

```python
import jax
import jax.numpy as jnp
from jax import lax

NY = 128
NZ = 8
FIELDS = 5
SPAN = 1
GROUPS = 4
NX = 512


def level_of(key, extent, cuts, smallest, top_value):
    def one(dim, blocks):
        draws = jax.random.uniform(jax.random.fold_in(jax.random.fold_in(key, 6), dim), (blocks,), jnp.float32, smallest / len(cuts), top_value / len(cuts))
        return jnp.repeat(jnp.exp(draws), extent[dim] // blocks).reshape((-1,) + (1,) * (len(extent) - dim - 1))

    loudness = one(*cuts[0])
    for cut in cuts[1:]:
        loudness = loudness * one(*cut)
    return loudness


def gaussian(rng, extent, deviation, limit, cuts=(), held_as=jnp.bfloat16):
    level = level_of(rng, extent, cuts, -0.22, 0.18) if cuts else 1.0
    array = jax.random.normal(rng, extent, jnp.float32) * deviation * level
    return jnp.minimum(jnp.maximum(array, -limit), limit).astype(held_as)


def setup_inputs(seed: int = 0) -> dict:
    key_of = jax.random.split(jax.random.key(seed), 3)
    return {
        "saved": gaussian(key_of[0], (GROUPS, FIELDS, NZ, NX, NY), 0.5, 2.5, ((0, 4), (3, 64)), jnp.float32),
        "sched": jax.random.permutation(key_of[1], GROUPS).astype(jnp.int32),
    }


time_step = 0.1
buoyancy_sq = 1.0
sound_sq = 1.0
hyper_coeff = 0.1

def slope_roll(field, along):
    near_diff = jnp.roll(field, -1, along) - jnp.roll(field, 1, along)
    far_diff = jnp.roll(field, -2, along) - jnp.roll(field, 2, along)
    return (8.0 * near_diff - far_diff) / 12.0

def hyper_roll(field, along):
    outer_sum = jnp.roll(field, -2, along) + jnp.roll(field, 2, along)
    inner_sum = jnp.roll(field, -1, along) + jnp.roll(field, 1, along)
    return outer_sum - 4.0 * inner_sum + 6.0 * field

def tendency(current):
    fields = [current[which] for which in range(5)]
    vel_x, vel_y, vel_z, buoy_field, press_field = fields

    def advect(field):
        return vel_x * slope_roll(field, 1) + vel_y * slope_roll(field, 2) + vel_z * slope_roll(field, 0)

    def smooth(field):
        return hyper_roll(field, 1) + hyper_roll(field, 2) + hyper_roll(field, 0)
    tend_u = -advect(vel_x) - slope_roll(press_field, 1) - hyper_coeff * smooth(vel_x)
    tend_v = -advect(vel_y) - slope_roll(press_field, 2) - hyper_coeff * smooth(vel_y)
    tend_w = -advect(vel_z) - slope_roll(press_field, 0) + buoy_field - hyper_coeff * smooth(vel_z)
    tend_b = -advect(buoy_field) - buoyancy_sq * vel_z - hyper_coeff * smooth(buoy_field)
    diverge = slope_roll(vel_x, 1) + slope_roll(vel_y, 2) + slope_roll(vel_z, 0)
    tend_p = -sound_sq * diverge - hyper_coeff * smooth(press_field)
    return jnp.stack([tend_u, tend_v, tend_w, tend_b, tend_p])

def advance(current):
    first = current + time_step * tendency(current)
    second = 0.75 * current + 0.25 * (first + time_step * tendency(first))
    return current / 3.0 + 2.0 / 3.0 * (second + time_step * tendency(second))

def reference(saved, sched):
    slot_ids = jnp.arange(GROUPS, dtype=jnp.int32)

    def start_of(cohort):
        position = jnp.sum(jnp.where(sched == cohort, slot_ids, 0)).astype(jnp.int32)
        return lax.dynamic_index_in_dim(saved, position, 0, keepdims=False)
    base_states = []
    current = start_of(0)
    for cohort in range(GROUPS - 1):
        current = start_of(cohort)
        for moment in range(SPAN):
            base_states.append(current)
            current = advance(current)
    adjoint = current - start_of(GROUPS - 1)
    for current in reversed(base_states):
        adjoint = jax.vjp(advance, current)[1](adjoint)[0]
    return adjoint
```

```python
import jax
import jax.numpy as jnp
from jax import lax
from jax.experimental import pallas as pl
from jax.experimental.pallas import tpu as pltpu
from jax.sharding import PartitionSpec as P

MESH = pl.DeviceIdType.MESH

DT = 0.1
HYPER = 0.1
HALO = 12
EDGE = 6
TILE = 8
ROWS = TILE + 2 * HALO
LROWS = TILE + 2 * EDGE
U, V, W, B, PR = range(5)

D8 = 8.0 / 12.0
D1 = 1.0 / 12.0
C1 = DT * HYPER
C4 = 4.0 * C1
C0 = 18.0 * C1


def lanes(v, k):
    return pltpu.roll(v, (-k) % 128, 1)


def planes(v, k):
    return pltpu.roll(v, (-k) % 8, 0)


def slope_parts(p1, m1, p2, m2):
    return D8 * (p1 - m1) - D1 * (p2 - m2)


def forward_row(src, i, slopes, want_rate):
    mid = [src[f, i] for f in range(5)]
    vel = mid[:3]
    rate = [None] * 5
    dxs, dys, dzs = [], [], []
    for f in range(5):
        q = mid[f]
        xp1, xm1, xp2, xm2 = src[f, i + 1], src[f, i - 1], src[f, i + 2], src[f, i - 2]
        yp1, ym1, yp2, ym2 = lanes(q, 1), lanes(q, -1), lanes(q, 2), lanes(q, -2)
        zp1, zm1, zp2, zm2 = planes(q, 1), planes(q, -1), planes(q, 2), planes(q, -2)
        dx = slope_parts(xp1, xm1, xp2, xm2)
        dy = slope_parts(yp1, ym1, yp2, ym2)
        dz = slope_parts(zp1, zm1, zp2, zm2)
        dxs.append(dx)
        dys.append(dy)
        dzs.append(dz)
        if slopes is not None and f < 4:
            slopes[f, i] = dx
            slopes[4 + f, i] = dy
            slopes[8 + f, i] = dz
        if want_rate:
            near = ((xp1 + xm1) + (yp1 + ym1)) + (zp1 + zm1)
            far = ((xp2 + xm2) + (yp2 + ym2)) + (zp2 + zm2)
            rate[f] = C4 * near - C1 * far - C0 * q
    if not want_rate:
        return None, None
    vd = [DT * c for c in vel]
    for f in range(4):
        rate[f] = rate[f] - (vd[0] * dxs[f] + vd[1] * dys[f] + vd[2] * dzs[f])
    rate[U] = rate[U] - DT * dxs[PR]
    rate[V] = rate[V] - DT * dys[PR]
    rate[W] = rate[W] - DT * (dzs[PR] - mid[B])
    rate[B] = rate[B] - vd[2]
    rate[PR] = rate[PR] - DT * ((dxs[U] + dys[V]) + dzs[W])
    return mid, rate


def transposed_row(adj, at, base, slopes, i):
    a = [adj[f, at] for f in range(5)]
    u_rows = {k: base[U, i + k] for k in (-2, -1, 1, 2)}
    u8p, u8m = (DT * D8) * u_rows[1], (DT * D8) * u_rows[-1]
    u1p, u1m = (DT * D1) * u_rows[2], (DT * D1) * u_rows[-2]
    v, w = base[V, i], base[W, i]
    v8, v1 = (DT * D8) * v, (DT * D1) * v
    w8, w1 = (DT * D8) * w, (DT * D1) * w
    ap = {k: adj[PR, at + k] for k in (-2, -1, 1, 2)}
    out = []
    for f in range(5):
        q = a[f]
        row = ap if f == PR else {k: adj[f, at + k] for k in (-2, -1, 1, 2)}
        total = C4 * (row[1] + row[-1]) - C1 * (row[2] + row[-2]) - C0 * q
        if f < 4:
            total = total + ((u8p * row[1] - u8m * row[-1]) - (u1p * row[2] - u1m * row[-2]))
            if f == U:
                total = total + ((DT * D8) * (ap[1] - ap[-1]) - (DT * D1) * (ap[2] - ap[-2]))
        else:
            au = {k: adj[U, at + k] for k in (-2, -1, 1, 2)}
            total = total + ((DT * D8) * (au[1] - au[-1]) - (DT * D1) * (au[2] - au[-2]))
        near, far = C4 * q, C1 * q
        if f < 4:
            p8, p1 = v8 * q, v1 * q
            if f == V:
                p8, p1 = p8 + (DT * D8) * a[PR], p1 + (DT * D1) * a[PR]
        else:
            p8, p1 = (DT * D8) * a[V], (DT * D1) * a[V]
        total = total + (lanes(near + p8, 1) + lanes(near - p8, -1))
        total = total - (lanes(far + p1, 2) + lanes(far - p1, -2))
        if f < 4:
            p8, p1 = w8 * q, w1 * q
            if f == W:
                p8, p1 = p8 + (DT * D8) * a[PR], p1 + (DT * D1) * a[PR]
        else:
            p8, p1 = (DT * D8) * a[W], (DT * D1) * a[W]
        total = total + (planes(near + p8, 1) + planes(near - p8, -1))
        total = total - (planes(far + p1, 2) + planes(far - p1, -2))
        out.append(total)
    ad = [DT * c for c in a[:4]]
    for d in range(3):
        s = ad[0] * slopes[4 * d, i] + ad[1] * slopes[4 * d + 1, i]
        s = s + (ad[2] * slopes[4 * d + 2, i] + ad[3] * slopes[4 * d + 3, i])
        out[d] = out[d] - s
    out[W] = out[W] - ad[3]
    out[B] = out[B] + ad[2]
    return a, out


def rows_loop(lo, hi, body):
    def step(j, carry):
        i = lo + 2 * j
        body(i)
        body(i + 1)
        return carry

    lax.fori_loop(0, (hi - lo) // 2, step, 0)


def first_stages(state, first, second, s0, s1, reach):
    def one(i):
        mid, rate = forward_row(state, i, s0, True)
        for f in range(5):
            first[f, i] = mid[f] + rate[f]

    rows_loop(HALO - reach - 2, HALO + TILE + reach + 2, one)

    def two(i):
        mid, rate = forward_row(first, i, s1, True)
        for f in range(5):
            second[f, i] = 0.75 * state[f, i] + 0.25 * (mid[f] + rate[f])

    rows_loop(HALO - reach, HALO + TILE + reach, two)


def last_slopes(second, s2):
    def three(i):
        forward_row(second, i, s2, False)

    rows_loop(HALO - 4, HALO + TILE + 4, three)


def misfit(state, second, s2, target, lam):
    def three(i):
        mid, rate = forward_row(second, i, s2, True)
        at = i - (HALO - EDGE)
        for f in range(5):
            end = state[f, i] / 3.0 + (2.0 / 3.0) * (mid[f] + rate[f])
            lam[f, at] = end - target[f, at]

    rows_loop(HALO - EDGE, HALO + TILE + EDGE, three)


def transposed_step(state, first, second, s0, s1, s2, lam, g2, g1, emit):
    shift = HALO - EDGE

    def three(i):
        a, out = transposed_row(lam, i - shift, second, s2, i)
        for f in range(5):
            g2[f, i - shift] = (2.0 / 3.0) * (a[f] + out[f])

    rows_loop(HALO - 4, HALO + TILE + 4, three)

    def two(i):
        a, out = transposed_row(g2, i - shift, first, s1, i)
        for f in range(5):
            g1[f, i - shift] = 0.25 * (a[f] + out[f])

    rows_loop(HALO - 2, HALO + TILE + 2, two)

    def one(i):
        at = i - shift
        a, out = transposed_row(g1, at, state, s0, i)
        for f in range(5):
            emit(f, i - HALO, lam[f, at] / 3.0 + 0.75 * g2[f, at] + (a[f] + out[f]))

    rows_loop(HALO, HALO + TILE, one)


def kernel(tiles, sched, saved, out, slots, ext, ext0, goal, first, second, slopes, first0, second0, slopes0, lam, lam1, done2, done1, g2, g1,
           own_sem, gs, gr, es, er, e0s, e0r, ts, tr, as_, ar, bs, br, fs, fr):
    sec, tile = lax.axis_index("section"), lax.axis_index("tile")
    core = lax.rem(sec, 2)
    mate = sec + 1 - 2 * core
    half = lax.div(sec, 2)
    across = sec + 2 - 4 * half
    near = {k: lax.rem(tile + tiles + k, tiles) for k in (-2, -1, 1, 2)}

    own = pltpu.make_async_copy(saved, slots.at[sec], own_sem)
    own.start()

    barrier = pltpu.get_barrier_semaphore()
    partners = [(mate, tile), (across, tile)] + [(sec, near[k]) for k in (-2, -1, 1, 2)] + [(mate, near[k]) for k in (-1, 1)]
    for who in partners:
        pl.semaphore_signal(barrier, inc=1, device_id=who, device_id_type=MESH)
    pl.semaphore_wait(barrier, len(partners))

    def send(src, dst, s, r, who):
        return pltpu.make_async_remote_copy(src_ref=src, dst_ref=dst, send_sem=s, recv_sem=r, device_id=who, device_id_type=MESH)

    to_across = send(saved, slots.at[sec], gs.at[0], gr.at[0], (across, tile))
    to_mate = send(saved, slots.at[sec], gs.at[1], gr.at[1], (mate, tile))
    to_across.start()
    to_mate.start()
    own.wait()
    to_across.wait_recv()
    relay = send(slots.at[across], slots.at[across], gs.at[2], gr.at[2], (mate, tile))
    relay.start()
    to_mate.wait_recv()
    relay.wait_recv()

    def slot_of(cohort):
        where = 0
        for j in range(1, 4):
            where = where + j * (sched[j] == cohort).astype(jnp.int32)
        return jnp.minimum(where, 3)

    def pick(which, dst, offset):
        def one(x, carry):
            for f in range(5):
                dst[f, offset + x] = slots[which, f, pl.ds(x, 8, stride=8), :]
            return carry

        lax.fori_loop(0, TILE, one, 0)

    def spread(buf, s, r, halo):
        copies = []
        reach = min(halo, TILE)
        lo, hi = halo, halo + TILE
        copies.append((1, send(buf.at[:, pl.ds(hi - reach, reach)], buf.at[:, pl.ds(halo - reach, reach)], s.at[0], r.at[0], (sec, near[1]))))
        copies.append((-1, send(buf.at[:, pl.ds(lo, reach)], buf.at[:, pl.ds(hi, reach)], s.at[1], r.at[1], (sec, near[-1]))))
        rest = halo - reach
        if rest:
            copies.append((2, send(buf.at[:, pl.ds(hi - rest, rest)], buf.at[:, pl.ds(0, rest)], s.at[2], r.at[2], (sec, near[2]))))
            copies.append((-2, send(buf.at[:, pl.ds(lo, rest)], buf.at[:, pl.ds(hi + reach, rest)], s.at[3], r.at[3], (sec, near[-2]))))
        for _, c in copies:
            c.start()
        return [c for _, c in copies]

    def hand_over(buf, dst, s, r):
        copies = [
            send(buf.at[:, pl.ds(TILE - EDGE, EDGE)], dst.at[:, pl.ds(0, EDGE)], s.at[0], r.at[0], (mate, near[1])),
            send(buf.at[:, pl.ds(0, EDGE)], dst.at[:, pl.ds(EDGE + TILE, EDGE)], s.at[1], r.at[1], (mate, near[-1])),
            send(buf, dst.at[:, pl.ds(EDGE, TILE)], s.at[2], r.at[2], (mate, tile)),
        ]
        return copies

    pick(core * slot_of(1) + (1 - core) * slot_of(2), ext, HALO)
    halo1 = spread(ext, es, er, HALO)
    s0, s1, s2 = slopes.at[0], slopes.at[1], slopes.at[2]
    z0, z1, z2 = slopes0.at[0], slopes0.at[1], slopes0.at[2]
    to_core1 = hand_over(done2, lam, as_, ar)
    to_core0 = hand_over(done1, lam1, bs, br)
    final = send(out, out, fs, fr, (mate, tile))

    @pl.when(core == 0)
    def _():
        pick(slot_of(3), goal, EDGE)
        halo_t = spread(goal, ts, tr, EDGE)
        pick(slot_of(0), ext0, HALO)
        halo0 = spread(ext0, e0s, e0r, HALO)
        for c in halo1:
            c.wait_recv()
        first_stages(ext, first, second, s0, s1, 8)
        for c in halo_t:
            c.wait_recv()
        misfit(ext, second, s2, goal, lam)

        def emit2(f, x, value):
            done2[f, x] = value

        transposed_step(ext, first, second, s0, s1, s2, lam, g2, g1, emit2)
        for c in to_core1:
            c.start()
        for c in halo0:
            c.wait_recv()
        first_stages(ext0, first0, second0, z0, z1, 6)
        last_slopes(second0, z2)
        for c in to_core0:
            c.wait_recv()

        def emit0(f, x, value):
            out[f, pl.ds(x, 8, stride=8), :] = value

        transposed_step(ext0, first0, second0, z0, z1, z2, lam1, g2, g1, emit0)
        final.start()
        for c in halo_t + halo0 + to_core1:
            c.wait_send()
        final.wait_send()

    @pl.when(core == 1)
    def _():
        for c in halo1:
            c.wait_recv()
        first_stages(ext, first, second, s0, s1, 6)
        last_slopes(second, s2)
        for c in to_core1:
            c.wait_recv()

        def emit1(f, x, value):
            done1[f, x] = value

        transposed_step(ext, first, second, s0, s1, s2, lam, g2, g1, emit1)
        for c in to_core0:
            c.start()
        for c in to_core0:
            c.wait_send()
        final.wait_recv()

    for c in halo1:
        c.wait_send()
    to_across.wait_send()
    to_mate.wait_send()
    relay.wait_send()


def solution(mesh):
    tiles = mesh.shape["tile"]

    def body(saved, sched):
        local = saved.reshape(5, 64, 128)
        f32 = jnp.float32
        state = pltpu.VMEM((5, ROWS, 8, 128), f32)
        margin = pltpu.VMEM((5, LROWS, 8, 128), f32)
        block = pltpu.VMEM((5, TILE, 8, 128), f32)
        dma = pltpu.SemaphoreType.DMA
        result = pl.pallas_call(
            lambda *refs: kernel(tiles, *refs),
            out_shape=jax.ShapeDtypeStruct((5, 64, 128), f32),
            in_specs=[pl.BlockSpec(memory_space=pltpu.SMEM), pl.BlockSpec(memory_space=pl.ANY)],
            out_specs=pl.BlockSpec(memory_space=pltpu.VMEM),
            scratch_shapes=[
                pltpu.VMEM((4, 5, 64, 128), f32),
                state, state, margin,
                state, state, pltpu.VMEM((3, 12, ROWS, 8, 128), f32),
                state, state, pltpu.VMEM((3, 12, ROWS, 8, 128), f32),
                margin, margin, block, block, margin, margin,
                dma, dma((3,)), dma((3,)), dma((4,)), dma((4,)), dma((4,)), dma((4,)),
                dma((2,)), dma((2,)), dma((3,)), dma((3,)), dma((3,)), dma((3,)), dma, dma,
            ],
            compiler_params=pltpu.CompilerParams(collective_id=0, has_side_effects=True, vmem_limit_bytes=48 * 1024 * 1024),
            name="adjoint",
        )(sched, local)
        return result.reshape(5, 8, 8, 128)

    placed = (P("section", None, None, "tile", None), P())
    return jax.shard_map(body, mesh=mesh, in_specs=placed, out_specs=P(None, None, "tile", None), check_vma=False)
```

```python
import jax
import jax.numpy as jnp
from jax import lax
from jax.experimental import pallas as pl
from jax.experimental.pallas import tpu as pltpu
from jax.sharding import PartitionSpec as P

MESH = pl.DeviceIdType.MESH

DT = 0.1
HYPER = 0.1
HALO = 6
TILE = 8
ROWS = TILE + 2 * HALO
U, V, W, B, PR = range(5)

D8 = 8.0 / 12.0
D1 = 1.0 / 12.0
C1 = DT * HYPER
C4 = 4.0 * C1
C0 = 18.0 * C1


def lanes(v, k):
    return pltpu.roll(v, (-k) % 128, 1)


def planes(v, k):
    return pltpu.roll(v, (-k) % 8, 0)


def slope_parts(p1, m1, p2, m2):
    return D8 * (p1 - m1) - D1 * (p2 - m2)


def forward_row(src, i, slopes, want_rate):
    mid = [src[f, i] for f in range(5)]
    vel = mid[:3]
    rate = [None] * 5
    dxs, dys, dzs = [], [], []
    for f in range(5):
        q = mid[f]
        xp1, xm1, xp2, xm2 = src[f, i + 1], src[f, i - 1], src[f, i + 2], src[f, i - 2]
        yp1, ym1, yp2, ym2 = lanes(q, 1), lanes(q, -1), lanes(q, 2), lanes(q, -2)
        zp1, zm1, zp2, zm2 = planes(q, 1), planes(q, -1), planes(q, 2), planes(q, -2)
        dx = slope_parts(xp1, xm1, xp2, xm2)
        dy = slope_parts(yp1, ym1, yp2, ym2)
        dz = slope_parts(zp1, zm1, zp2, zm2)
        dxs.append(dx)
        dys.append(dy)
        dzs.append(dz)
        if slopes is not None and f < 4:
            slopes[f, i] = dx
            slopes[4 + f, i] = dy
            slopes[8 + f, i] = dz
        if want_rate:
            near = ((xp1 + xm1) + (yp1 + ym1)) + (zp1 + zm1)
            far = ((xp2 + xm2) + (yp2 + ym2)) + (zp2 + zm2)
            rate[f] = C4 * near - C1 * far - C0 * q
    if not want_rate:
        return None, None
    vd = [DT * c for c in vel]
    for f in range(4):
        rate[f] = rate[f] - (vd[0] * dxs[f] + vd[1] * dys[f] + vd[2] * dzs[f])
    rate[U] = rate[U] - DT * dxs[PR]
    rate[V] = rate[V] - DT * dys[PR]
    rate[W] = rate[W] - DT * (dzs[PR] - mid[B])
    rate[B] = rate[B] - vd[2]
    rate[PR] = rate[PR] - DT * ((dxs[U] + dys[V]) + dzs[W])
    return mid, rate


def transposed_row(adj, base, slopes, i):
    at = i
    a = [adj[f, at] for f in range(5)]
    u_rows = {k: base[U, i + k] for k in (-2, -1, 1, 2)}
    u8p, u8m = (DT * D8) * u_rows[1], (DT * D8) * u_rows[-1]
    u1p, u1m = (DT * D1) * u_rows[2], (DT * D1) * u_rows[-2]
    v, w = base[V, i], base[W, i]
    v8, v1 = (DT * D8) * v, (DT * D1) * v
    w8, w1 = (DT * D8) * w, (DT * D1) * w
    ap = {k: adj[PR, at + k] for k in (-2, -1, 1, 2)}
    out = []
    for f in range(5):
        q = a[f]
        row = ap if f == PR else {k: adj[f, at + k] for k in (-2, -1, 1, 2)}
        total = C4 * (row[1] + row[-1]) - C1 * (row[2] + row[-2]) - C0 * q
        if f < 4:
            total = total + ((u8p * row[1] - u8m * row[-1]) - (u1p * row[2] - u1m * row[-2]))
            if f == U:
                total = total + ((DT * D8) * (ap[1] - ap[-1]) - (DT * D1) * (ap[2] - ap[-2]))
        else:
            au = {k: adj[U, at + k] for k in (-2, -1, 1, 2)}
            total = total + ((DT * D8) * (au[1] - au[-1]) - (DT * D1) * (au[2] - au[-2]))
        near, far = C4 * q, C1 * q
        if f < 4:
            p8, p1 = v8 * q, v1 * q
            if f == V:
                p8, p1 = p8 + (DT * D8) * a[PR], p1 + (DT * D1) * a[PR]
        else:
            p8, p1 = (DT * D8) * a[V], (DT * D1) * a[V]
        total = total + (lanes(near + p8, 1) + lanes(near - p8, -1))
        total = total - (lanes(far + p1, 2) + lanes(far - p1, -2))
        if f < 4:
            p8, p1 = w8 * q, w1 * q
            if f == W:
                p8, p1 = p8 + (DT * D8) * a[PR], p1 + (DT * D1) * a[PR]
        else:
            p8, p1 = (DT * D8) * a[W], (DT * D1) * a[W]
        total = total + (planes(near + p8, 1) + planes(near - p8, -1))
        total = total - (planes(far + p1, 2) + planes(far - p1, -2))
        out.append(total)
    ad = [DT * c for c in a[:4]]
    for d in range(3):
        s = ad[0] * slopes[4 * d, i] + ad[1] * slopes[4 * d + 1, i]
        s = s + (ad[2] * slopes[4 * d + 2, i] + ad[3] * slopes[4 * d + 3, i])
        out[d] = out[d] - s
    out[W] = out[W] - ad[3]
    out[B] = out[B] + ad[2]
    return a, out


def margin_row(adj, base, i, offsets):
    out = [None] * 5
    for k in offsets:
        near = abs(k) == 1
        size = D8 if near else -D1
        slope = DT * size if k > 0 else -DT * size
        hyper = C4 if near else -C1
        a = [adj[f, i + k] for f in range(5)]
        speed = slope * base[U, i + k] + hyper
        for f in range(5):
            term = speed * a[f] if f < 4 else hyper * a[f]
            if f == U:
                term = term + slope * a[PR]
            if f == PR:
                term = term + slope * a[U]
            out[f] = term if out[f] is None else out[f] + term
    return out


def margins(adj, base, lo, hi, put):
    for i, offsets in ((lo - 2, (2,)), (lo - 1, (1, 2)), (hi, (-1, -2)), (hi + 1, (-2,))):
        put(i, margin_row(adj, base, i, offsets))


def rows_loop(lo, hi, body):
    def step(j, carry):
        i = lo + 2 * j
        body(i)
        body(i + 1)
        return carry

    lax.fori_loop(0, (hi - lo) // 2, step, 0)


LO, HI = HALO, HALO + TILE


def first_stages(state, first, second, s0, s1):
    def one(i):
        mid, rate = forward_row(state, i, s0, True)
        for f in range(5):
            first[f, i] = mid[f] + rate[f]

    rows_loop(LO - 4, HI + 4, one)

    def two(i):
        mid, rate = forward_row(first, i, s1, True)
        for f in range(5):
            second[f, i] = 0.75 * state[f, i] + 0.25 * (mid[f] + rate[f])

    rows_loop(LO - 2, HI + 2, two)


def last_slopes(second, s2):
    def three(i):
        forward_row(second, i, s2, False)

    rows_loop(LO, HI, three)


def misfit(state, second, s2, slots, goal, lam):
    def three(i):
        mid, rate = forward_row(second, i, s2, True)
        for f in range(5):
            end = state[f, i] / 3.0 + (2.0 / 3.0) * (mid[f] + rate[f])
            lam[f, i] = end - slots[goal, f, pl.ds(i - LO, 8, stride=8), :]

    rows_loop(LO, HI, three)


def clear(buf, width):
    for f in range(5):
        for i in range(width):
            buf[f, i] = jnp.zeros((8, 128), jnp.float32)
            buf[f, ROWS - 1 - i] = jnp.zeros((8, 128), jnp.float32)


def transposed_step(state, first, second, s0, s1, s2, lam, g2, g1, gq, edges_done):
    def three(i):
        a, out = transposed_row(lam, second, s2, i)
        for f in range(5):
            g2[f, i] = (2.0 / 3.0) * (a[f] + out[f])

    def put2(i, out):
        for f in range(5):
            g2[f, i] = (2.0 / 3.0) * out[f]

    margins(lam, second, LO, HI, put2)
    rows_loop(LO, HI, three)

    def two(i):
        a, out = transposed_row(g2, first, s1, i)
        for f in range(5):
            g1[f, i] = 0.25 * (a[f] + out[f])

    def put1(i, out):
        for f in range(5):
            g1[f, i] = 0.25 * out[f]

    margins(g2, first, LO - 2, HI + 2, put1)
    rows_loop(LO - 2, HI + 2, two)

    def one(i):
        a, out = transposed_row(g1, state, s0, i)
        for f in range(5):
            gq[f, i] = lam[f, i] / 3.0 + 0.75 * g2[f, i] + (a[f] + out[f])

    def put0(i, out):
        for f in range(5):
            gq[f, i] = out[f]

    margins(g1, state, LO - 4, HI + 4, put0)

    def edge(j, carry):
        one(LO - 4 + j)
        one(HI + j)
        return carry

    lax.fori_loop(0, 4, edge, 0)
    edges_done()
    rows_loop(LO, HI, one)


def collect(parts, put):
    middle, before, after = parts
    for x in range(TILE):
        for f in range(5):
            total = middle(f, x)
            if x < HALO:
                total = total + before[f, x]
            if x >= TILE - HALO:
                total = total + after[f, x - (TILE - HALO)]
            put(f, x, total)


def kernel(tiles, sched_in, saved, out, sched, sched_sem, slots, ext, ext0, first, second, slopes, first0, second0, slopes0, lam, g2, g1, gq, gq0,
           mid_in, mid_last, before_in, after_in, before_last, after_last,
           own_sem, gs, gr, es, er, e0s, e0r, as_, ar, fs, fr, go):
    sec, tile = lax.axis_index("section"), lax.axis_index("tile")
    core = lax.rem(sec, 2)
    mate = sec + 1 - 2 * core
    half = lax.div(sec, 2)
    across = sec + 2 - 4 * half
    right, left = lax.rem(tile + 1, tiles), lax.rem(tile + tiles - 1, tiles)

    own = pltpu.make_async_copy(saved, slots.at[sec], own_sem)
    own.start()
    order = pltpu.make_async_copy(sched_in, sched, sched_sem)
    order.start()

    barrier = pltpu.get_barrier_semaphore()
    partners = [(mate, tile), (across, tile), (sec, left), (sec, right), (mate, left), (mate, right)]
    for who in partners:
        pl.semaphore_signal(barrier, inc=1, device_id=who, device_id_type=MESH)
    clear(lam, 6)
    clear(g2, 4)
    clear(g1, 2)
    pl.semaphore_wait(barrier, len(partners))

    def send(src, dst, s, r, who):
        return pltpu.make_async_remote_copy(src_ref=src, dst_ref=dst, send_sem=s, recv_sem=r, device_id=who, device_id_type=MESH)

    to_across = send(saved, slots.at[sec], gs.at[0], gr.at[0], (across, tile))
    to_mate = send(saved, slots.at[sec], gs.at[1], gr.at[1], (mate, tile))
    to_across.start()
    to_mate.start()
    own.wait()
    order.wait()
    to_across.wait_recv()
    relay = send(slots.at[across], slots.at[across], gs.at[2], gr.at[2], (mate, tile))
    relay.start()
    to_mate.wait_recv()
    relay.wait_recv()

    def slot_of(cohort):
        where = 0
        for j in range(1, 4):
            where = where + j * (sched[j] == cohort).astype(jnp.int32)
        return jnp.minimum(where, 3)

    def pick(which, dst):
        def one(x, carry):
            for f in range(5):
                dst[f, LO + x] = slots[which, f, pl.ds(x, 8, stride=8), :]
            return carry

        lax.fori_loop(0, TILE, one, 0)

    def spread(buf, s, r):
        copies = [
            send(buf.at[:, pl.ds(HI - HALO, HALO)], buf.at[:, pl.ds(0, HALO)], s.at[0], r.at[0], (sec, right)),
            send(buf.at[:, pl.ds(LO, HALO)], buf.at[:, pl.ds(HI, HALO)], s.at[1], r.at[1], (sec, left)),
        ]
        return copies

    def push_edges(buf, before, after, s, r, to, k):
        return [
            send(buf.at[:, pl.ds(HI, HALO)], before, s.at[k], r.at[k], (to, right)),
            send(buf.at[:, pl.ds(0, HALO)], after, s.at[k + 1], r.at[k + 1], (to, left)),
        ]

    def start(copies):
        for c in copies:
            c.start()

    def received(copies):
        for c in copies:
            c.wait_recv()

    def sent(copies):
        for c in copies:
            c.wait_send()

    s0, s1, s2 = slopes.at[0], slopes.at[1], slopes.at[2]
    z0, z1, z2 = slopes0.at[0], slopes0.at[1], slopes0.at[2]
    halo1, halo0 = spread(ext, es, er), spread(ext0, e0s, e0r)
    edges = push_edges(gq, before_in, after_in, as_, ar, mate, 0)
    centre = send(gq.at[:, pl.ds(LO, TILE)], mid_in, as_.at[2], ar.at[2], (mate, tile))
    last_own = push_edges(gq0, before_last, after_last, fs, fr, sec, 0)
    last_mate = push_edges(gq0, before_last, after_last, fs, fr, mate, 2)
    last_centre = send(gq0.at[:, pl.ds(LO, TILE)], mid_last, fs.at[4], fr.at[4], (mate, tile))

    def put_lam(f, x, value):
        lam[f, LO + x] = value

    def put_out(f, x, value):
        out[f, pl.ds(x, 8, stride=8), :] = value

    pick(core * slot_of(1) + (1 - core) * slot_of(2), ext)

    @pl.when(core == 0)
    def _():
        start(halo1)
        pick(slot_of(0), ext0)
        received(halo1)
        sent(halo1)
        pl.semaphore_signal(go, inc=1, device_id=(mate, tile), device_id_type=MESH)
        start(halo0)
        first_stages(ext, first, second, s0, s1)
        misfit(ext, second, s2, slots, slot_of(3), lam)
        transposed_step(ext, first, second, s0, s1, s2, lam, g2, g1, gq, lambda: start(edges))
        centre.start()
        received(halo0)
        first_stages(ext0, first0, second0, z0, z1)
        last_slopes(second0, z2)
        received(edges + [centre])
        collect((lambda f, x: mid_in[f, x], before_in, after_in), put_lam)
        transposed_step(ext0, first0, second0, z0, z1, z2, lam, g2, g1, gq0, lambda: start(last_own + last_mate))
        last_centre.start()
        received(last_own)
        collect((lambda f, x: gq0[f, LO + x], before_last, after_last), put_out)
        sent(halo0 + edges + [centre] + last_own + last_mate + [last_centre])

    @pl.when(core == 1)
    def _():
        pl.semaphore_wait(go, 1)
        start(halo1)
        received(halo1)
        first_stages(ext, first, second, s0, s1)
        last_slopes(second, s2)
        received(edges + [centre])
        collect((lambda f, x: mid_in[f, x], before_in, after_in), put_lam)
        transposed_step(ext, first, second, s0, s1, s2, lam, g2, g1, gq, lambda: start(edges))
        centre.start()
        received(last_mate + [last_centre])
        collect((lambda f, x: mid_last[f, x], before_last, after_last), put_out)
        sent(halo1 + edges + [centre])

    sent([to_across, to_mate, relay])


def solution(mesh):
    tiles = mesh.shape["tile"]

    def body(saved, sched):
        local = saved.reshape(5, 64, 128)
        f32 = jnp.float32
        state = pltpu.VMEM((5, ROWS, 8, 128), f32)
        block = pltpu.VMEM((5, TILE, 8, 128), f32)
        margin = pltpu.VMEM((5, HALO, 8, 128), f32)
        slopes = pltpu.VMEM((3, 12, ROWS, 8, 128), f32)
        dma = pltpu.SemaphoreType.DMA
        result = pl.pallas_call(
            lambda *refs: kernel(tiles, *refs),
            out_shape=jax.ShapeDtypeStruct((5, 64, 128), f32),
            in_specs=[pl.BlockSpec(memory_space=pltpu.HBM), pl.BlockSpec(memory_space=pltpu.HBM)],
            out_specs=pl.BlockSpec(memory_space=pltpu.VMEM),
            scratch_shapes=[
                pltpu.SMEM((4,), jnp.int32), pltpu.SemaphoreType.DMA,
                pltpu.VMEM((4, 5, 64, 128), f32),
                state, state, state, state, slopes, state, state, slopes,
                state, state, state, state, state,
                block, block, margin, margin, margin, margin,
                dma, dma((3,)), dma((3,)), dma((2,)), dma((2,)), dma((2,)), dma((2,)),
                dma((3,)), dma((3,)), dma((5,)), dma((5,)), pltpu.SemaphoreType.REGULAR,
            ],
            compiler_params=pltpu.CompilerParams(collective_id=0, has_side_effects=True, vmem_limit_bytes=48 * 1024 * 1024),
            name="adjoint",
        )(sched, local)
        return result.reshape(5, 8, 8, 128)

    placed = (P("section", None, None, "tile", None), P())
    return jax.shard_map(body, mesh=mesh, in_specs=placed, out_specs=P(None, None, "tile", None), check_vma=False)
```
